512 devices in a mesh: row: 16 (over y, x), col: 32 (over z, core).
Axes of the slice: x: 4, y: 4, z: 16, core: 2. Of those that a mesh axis runs over, the one named last changes fastest.
Arguments:
- sources: bfloat16 [131072, 1024], P(('row', 'col')), may hold values from -6 to 6
- leaf_in: bfloat16 [512, 256, 256], P(('row', 'col')), may hold values from -0.375 to 0.375
- transfers: bfloat16 [512, 9, 2, 256, 256], P(('row', 'col')), may hold values from -0.25 to 0.25
- leaf_out: bfloat16 [512, 256, 256], P(('row', 'col')), may hold values from -0.375 to 0.375
- tile_mats: bfloat16 [512, 5, 256, 256], P(('row', 'col')), may hold values from -0.375 to 0.375
- tile_list: int32 [512, 5], P(('row', 'col')), may hold values from 0 to 1, as said below
Outputs:
- applied: bfloat16 [131072, 1024], P(('row', 'col'))
The draws below stay inside these ranges and needn't reach their ends.
Inputs may be any that keep to these rules, and one draw needn't show every extreme that they name: tile_list[b, k] is 1 where source block b holds a tile onto the block k - 2 places further along its row of 32 blocks; always 1 for k = 2, always 0 where that block lies outside the row; blocks hold different numbers of tiles.
All inputs are finite; a program needn't handle non-finite values.
Results may differ from the reference program's by a relative error of at most 0.015.
Values may be sent and summed in bfloat16 or wider, within the bound.
No kernel may reach another device: no remote copies, remote signals or barrier semaphores. Data moves between devices by JAX's collectives and lax.ppermute only.
A program may use at most 64 MiB of HBM per device.

```python
import jax
import jax.numpy as jnp

RANK = 256
VECS = 1024
TILES = 5
BLOCKS = 512
COL_BLOCKS = 32
LROW = 4
LCOL = 5
LEVELS = 9
N_ROW = 16
N_COL = 32


def draw_tile_list(key, part):
    base = jax.random.fold_in(key, 11)
    first, second = jax.random.split(base)
    level = jax.random.randint(first, (BLOCKS, 1), 1, 5)
    rolled = jax.random.randint(second, (BLOCKS, TILES), 0, 4)
    live = (rolled < level).astype(jnp.int32)
    column = (jnp.arange(BLOCKS, dtype=jnp.int32) % COL_BLOCKS)[:, None]
    offsets = jnp.arange(TILES, dtype=jnp.int32)[None, :] - TILES // 2
    target = column + offsets
    inside = (target >= 0) & (target < COL_BLOCKS)
    live = jnp.where(inside, live, 0)
    live = jnp.where(offsets == 0, 1, live)
    return live.astype(jnp.int32)


def block_scale(rng, extent, cuts, low, top_value):
    loudness, own = 1.0, jax.random.fold_in(rng, 6)
    for position, parts in cuts:
        draws = jnp.exp(jax.random.uniform(jax.random.fold_in(own, position), (parts,), jnp.float32, low / len(cuts), top_value / len(cuts)))
        loudness = loudness * jnp.repeat(draws, extent[position] // parts).reshape([-1 if axis == position else 1 for axis in range(len(extent))])
    return loudness


def noise(stream_key, extent, deviation, reach, pieces=(), held_as=jnp.bfloat16):
    result = jax.random.normal(stream_key, extent, jnp.float32) * deviation
    if len(pieces) > 0:
        result = block_scale(stream_key, extent, pieces, -0.22, 0.18) * result
    return jnp.clip(result, min=-reach, max=reach).astype(held_as)


def setup_inputs(seed: int = 0) -> dict:
    seeds = jax.random.split(jax.random.key(seed), 7)
    return {
        "sources": noise(seeds[0], (BLOCKS * RANK, VECS), 1.0, 6.0, ((0, 512),)),
        "leaf_in": noise(seeds[1], (BLOCKS, RANK, RANK), RANK ** -0.5, 0.375, ((0, 512),)),
        "transfers": noise(seeds[2], (BLOCKS, LEVELS, 2, RANK, RANK), (2 * RANK) ** -0.5, 0.25, ((0, 512),)),
        "leaf_out": noise(seeds[3], (BLOCKS, RANK, RANK), RANK ** -0.5, 0.375, ((0, 512),)),
        "tile_mats": noise(seeds[4], (BLOCKS, TILES, RANK, RANK), RANK ** -0.5, 0.375, ((0, 512),)),
        "tile_list": draw_tile_list(jax.random.fold_in(seeds[6], 71), 0),
    }


def batch_mul(mats, vecs):
    return jnp.einsum("bij,bjv->biv", mats.astype(jnp.float32), vecs.astype(jnp.float32))


def partner_of(coeffs, bit):
    shaped = coeffs.reshape(BLOCKS // (2 ** (bit + 1)), 2, 2 ** bit, RANK, VECS)
    return shaped[:, ::-1].reshape(BLOCKS, RANK, VECS)


def shift_cols(values, offset):
    grid = values.reshape(N_ROW, N_COL, RANK, VECS)
    if offset > 0:
        grid = jnp.pad(grid, ((0, 0), (offset, 0), (0, 0), (0, 0)))[:, :N_COL]
    elif offset < 0:
        grid = jnp.pad(grid, ((0, 0), (0, -offset), (0, 0), (0, 0)))[:, -offset:]
    return grid.reshape(BLOCKS, RANK, VECS)


def reference(sources, leaf_in, transfers, leaf_out, tile_mats, tile_list):
    blocks = sources.reshape(BLOCKS, RANK, VECS)
    coeffs = batch_mul(leaf_in, blocks).astype(jnp.bfloat16)
    for level in range(LEVELS):
        if level < LROW:
            bit = LCOL + level
        else:
            bit = level - LROW
        partner = partner_of(coeffs, bit)
        mixed = batch_mul(transfers[:, level, 0], coeffs) + batch_mul(transfers[:, level, 1], partner)
        coeffs = mixed.astype(jnp.bfloat16)
    far = batch_mul(leaf_out, coeffs)
    live = tile_list.astype(jnp.float32)
    near = jnp.zeros((BLOCKS, RANK, VECS), jnp.float32)
    for k in range(TILES):
        product = batch_mul(tile_mats[:, k], blocks) * live[:, k][:, None, None]
        near = near + shift_cols(product, k - TILES // 2)
    return (far + near).astype(jnp.bfloat16).reshape(BLOCKS * RANK, VECS)
```

```python
import jax
import jax.numpy as jnp
from jax import lax
from jax.sharding import PartitionSpec as P

TILES = 5
CHUNKS = 2


def exchange(block, axis, flip):
    count = lax.axis_size(axis)
    return lax.ppermute(block, axis, [(i, i ^ flip) for i in range(count)])


def from_behind(shard, axis, by):
    devices = lax.axis_size(axis)
    pairs = [(i, i + by) for i in range(devices) if 0 <= i + by < devices]
    return lax.ppermute(shard, axis, pairs)


def mixing(mats, vectors):
    return jnp.dot(mats, vectors, preferred_element_type=jnp.float32)


def mixed(own_mat, partner_mat, own, partner):
    return (mixing(own_mat, own) + mixing(partner_mat, partner)).astype(jnp.bfloat16)


def shards(sources, leaf_in, transfers, leaf_out, tile_mats, tile_list):
    levels_high = lax.axis_size("row").bit_length() - 1
    levels_low = lax.axis_size("col").bit_length() - 1
    hops = [("row", 1 << bit) for bit in range(levels_high)]
    hops += [("col", 1 << bit) for bit in range(levels_low)]
    last = len(hops) - 1
    top, below = hops[last][1], hops[last - 1][1]
    width = sources.shape[1] // CHUNKS
    parts = [sources[:, i * width : (i + 1) * width] for i in range(CHUNKS)]

    partner_mats = exchange(transfers[0, last - 1], "col", below)

    coeffs = [mixing(leaf_in[0], part).astype(jnp.bfloat16) for part in parts]

    def ordinary(level, own):
        axis, flip = hops[level]
        partner = exchange(own, axis, flip)
        return mixed(transfers[0, level, 0], transfers[0, level, 1], own, partner)

    def last_two(own):
        partner = exchange(own, "col", below)
        for_other = mixed(partner_mats[0], partner_mats[1], partner, own)
        from_other = exchange(for_other, "col", top ^ below)
        own = mixed(transfers[0, last - 1, 0], transfers[0, last - 1, 1], own, partner)
        return mixed(transfers[0, last, 0], transfers[0, last, 1], own, from_other)

    for step in range(last + CHUNKS):
        for i in range(CHUNKS):
            level = step - i
            if 0 <= level < last - 1:
                coeffs[i] = ordinary(level, coeffs[i])
            elif level == last - 1:
                coeffs[i] = last_two(coeffs[i])

    live = tile_list[0].astype(jnp.float32)
    middle = TILES // 2
    near = live[middle] * mixing(tile_mats[0, middle], sources)
    for k in range(TILES):
        if k == middle:
            continue
        product = live[k] * mixing(tile_mats[0, k], sources)
        near = near + from_behind(product.astype(jnp.bfloat16), "col", k - middle).astype(
            product.dtype
        )
    out = [
        (mixing(leaf_out[0], coeffs[i]) + near[:, i * width : (i + 1) * width]).astype(jnp.bfloat16)
        for i in range(CHUNKS)
    ]
    return jnp.concatenate(out, axis=1)


def solution(mesh):
    return jax.shard_map(
        shards,
        mesh=mesh,
        in_specs=(
            P(("row", "col"), None),
            P(("row", "col"), None, None),
            P(("row", "col"), None, None, None, None),
            P(("row", "col"), None, None),
            P(("row", "col"), None, None, None),
            P(("row", "col"), None),
        ),
        out_specs=P(("row", "col"), None),
        check_vma=False,
    )
```

```python
import jax
import jax.numpy as jnp
from jax import lax
from jax.sharding import PartitionSpec as P


TILES = 5


def exchange(block, axis, flip):
    count = lax.axis_size(axis)
    return lax.ppermute(block, axis, [(i, i ^ flip) for i in range(count)])


def from_behind(shard, axis, by):
    devices = lax.axis_size(axis)
    pairs = [(i, i + by) for i in range(devices) if 0 <= i + by < devices]
    return lax.ppermute(shard, axis, pairs)


def mixing(mats, vectors):
    return jnp.dot(mats, vectors, preferred_element_type=jnp.float32)


def two(first_mat, second_mat, first, second):
    return mixing(first_mat, first) + mixing(second_mat, second)


def rounded(values):
    return values.astype(jnp.bfloat16)


class Pair:
    def __init__(self, axis, low, high, level, transfers):
        self.axis, self.low, self.side, self.high = axis, low, low ^ high, high
        self.first, self.second = transfers[0, level], transfers[0, level + 1]
        self.both = transfers[0, level : level + 2]

    def fetch(self):
        both = self.both
        self.near = exchange(both, self.axis, self.low)
        self.at_side = exchange(both[0, 0], self.axis, self.side)
        self.at_far = exchange(both[0, 1], self.axis, self.high)

    def run(self, coeffs):
        half = coeffs.shape[1] // 2
        one, other = coeffs[:, :half], coeffs[:, half:]
        low = exchange(one, self.axis, self.low)
        side = exchange(other, self.axis, self.side)

        passed = exchange(rounded(two(self.near[0, 0], self.near[0, 1], low, one)), self.axis, self.side)
        mine = rounded(two(self.first[0], self.first[1], one, low))

        part = two(
            self.near[1, 0],
            self.near[1, 1],
            rounded(mixing(self.near[0, 1], other)),
            rounded(mixing(self.at_side, side)),
        )
        added = exchange(rounded(part), self.axis, self.low)
        own = two(
            self.second[0],
            self.second[1],
            rounded(mixing(self.first[0], other)),
            rounded(mixing(self.at_far, side)),
        )
        return [
            rounded(two(self.second[0], self.second[1], mine, passed)),
            rounded(own + added.astype(jnp.float32)),
        ]


def near_field(sources, tile_mats, live):
    products = [live[k] * mixing(tile_mats[0, k], sources) for k in range(TILES)]
    core = lax.axis_index("col") % 2
    steps = jnp.stack([rounded(products[1]), rounded(products[3])])
    down, up = exchange(steps, "col", 1).astype(jnp.float32)
    first = core == 0
    above = from_behind(rounded(products[4] + jnp.where(first, up, 0.0)), "col", 2)
    beneath = from_behind(rounded(products[0] + jnp.where(first, 0.0, down)), "col", -2)
    near = products[2] + jnp.where(first, down, up)
    return near + above.astype(jnp.float32) + beneath.astype(jnp.float32)


def shards(sources, leaf_in, transfers, leaf_out, tile_mats, tile_list):
    levels_high = lax.axis_size("row").bit_length() - 1
    levels_low = lax.axis_size("col").bit_length() - 1
    hops = [("row", 1 << bit) for bit in range(levels_high)]
    hops += [("col", 1 << bit) for bit in range(levels_low)]
    last = len(hops) - 1
    live = tile_list[0].astype(jnp.float32)

    def ordinary(level, own):
        axis, flip = hops[level]
        partner = exchange(own, axis, flip)
        return rounded(two(transfers[0, level, 0], transfers[0, level, 1], own, partner))

    outer = Pair("col", hops[last - 1][1], hops[last][1], last - 1, transfers)
    coeffs = rounded(mixing(leaf_in[0], sources))
    outer.fetch()
    coeffs = ordinary(0, coeffs)
    near = near_field(sources, tile_mats, live)
    for level in range(1, last - 1):
        coeffs = ordinary(level, coeffs)
    halves = outer.run(coeffs)
    half = halves[0].shape[1]
    out = [
        rounded(mixing(leaf_out[0], part) + near[:, i * half : (i + 1) * half])
        for i, part in enumerate(halves)
    ]
    return jnp.concatenate(out, axis=1)


def solution(mesh):
    return jax.shard_map(
        shards,
        mesh=mesh,
        in_specs=(
            P(("row", "col"), None),
            P(("row", "col"), None, None),
            P(("row", "col"), None, None, None, None),
            P(("row", "col"), None, None),
            P(("row", "col"), None, None, None),
            P(("row", "col"), None),
        ),
        out_specs=P(("row", "col"), None),
        check_vma=False,
    )
```

```python
import jax
import jax.numpy as jnp
from jax import lax
from jax.experimental import pallas as pl
from jax.experimental.pallas import tpu as pltpu
from jax.sharding import PartitionSpec as P


TILE = 256
VMEM = pl.BlockSpec(memory_space=pltpu.VMEM)
SMEM = pl.BlockSpec(memory_space=pltpu.SMEM)


def exchange(block, axis, flip):
    count = lax.axis_size(axis)
    return lax.ppermute(block, axis, [(i, i ^ flip) for i in range(count)])


def from_behind(shard, axis, by):
    devices = lax.axis_size(axis)
    pairs = [(i, i + by) for i in range(devices) if 0 <= i + by < devices]
    return lax.ppermute(shard, axis, pairs)


def mixing(mats, vectors):
    return jnp.dot(mats, vectors, preferred_element_type=jnp.float32)


def rounded(values):
    return values.astype(jnp.bfloat16)


def columns(ref_width):
    return [slice(i, i + TILE) for i in range(0, ref_width, TILE)]


def local(body, outs, ins, products, width=None):
    shapes = [jax.ShapeDtypeStruct(shape, dtype) for shape, dtype in outs]
    moved = sum(x.size * x.dtype.itemsize for x in [*ins, *shapes])

    def spec(x):
        if x.size < 16:
            return SMEM
        if width is None:
            return VMEM
        lead = len(x.shape) - 1
        if x.shape[-1] == width:
            return pl.BlockSpec((*x.shape[:-1], TILE), lambda i: (0,) * lead + (i,))
        return pl.BlockSpec(x.shape, lambda i: (0,) * (lead + 1))

    return pl.pallas_call(
        body,
        out_shape=shapes,
        grid=() if width is None else (width // TILE,),
        in_specs=[spec(x) for x in ins],
        out_specs=[spec(x) for x in shapes],
        compiler_params=pltpu.CompilerParams(vmem_limit_bytes=8 << 20),
        cost_estimate=pl.CostEstimate(flops=products * 2**25, bytes_accessed=moved, transcendentals=0),
    )(*ins)


def near_products(live, tiles, sources, steps):
    block = sources[...]
    steps[0] = rounded(live[0, 1] * mixing(tiles[0, 1], block))
    steps[1] = rounded(live[0, 3] * mixing(tiles[0, 3], block))


def near_meet(core, live, tiles, sources, met, down, up):
    block = sources[...]
    lowest = live[0, 0] * mixing(tiles[0, 0], block)
    highest = live[0, 4] * mixing(tiles[0, 4], block)
    first = core[0] == 0
    down[...] = rounded(lowest + jnp.where(first, 0.0, met[0].astype(jnp.float32)))
    up[...] = rounded(highest + jnp.where(first, met[1].astype(jnp.float32), 0.0))


def pair_ready(near, at_side, one, other, ready_one, ready_other, across, first):
    first[...] = near[0, 0]
    across[...] = rounded(mixing(near[1, 1], at_side[0]))
    for cols in columns(one.shape[1]):
        ready_one[:, cols] = mixing(near[0, 1], one[:, cols])
        ready_other[:, cols] = mixing(near[1, 0], rounded(mixing(near[0, 1], other[:, cols])))


def pair_send(mat, ready, arrived, sent):
    for cols in columns(arrived.shape[1]):
        sent[:, cols] = rounded(ready[:, cols] + mixing(mat[...], arrived[:, cols]))


def finish_base(level):
    def body(core, live, transfers, leaf_out, at_side, tiles, one, low, other, side, sources, met, above, beneath, base_one, base_other, out_second):
        out = leaf_out[0]
        first, second = transfers[0, level], transfers[0, level + 1]
        out_second[...] = rounded(mixing(out, second[1]))
        half = one.shape[1]
        for cols in columns(half):
            mine = rounded(mixing(first[0], one[:, cols]) + mixing(first[1], low[:, cols]))
            base_one[:, cols] = mixing(out, rounded(mixing(second[0], mine)))
            own = mixing(second[0], rounded(mixing(first[0], other[:, cols])))
            own = own + mixing(second[1], rounded(mixing(at_side[1], side[:, cols])))
            base_other[:, cols] = mixing(out, rounded(own))
        for base, start in ((base_one, 0), (base_other, half)):
            for cols in columns(half):
                at = slice(start + cols.start, start + cols.stop)
                near = live[0, 2] * mixing(tiles[0, 2], sources[:, at])
                near = near + above[:, at].astype(jnp.float32) + beneath[:, at].astype(jnp.float32)
                step = jnp.where(core[0] == 0, met[0, :, at], met[1, :, at])
                base[:, cols] = base[:, cols] + near + step.astype(jnp.float32)

    return body


def finish(out_second, leaf_out, base_one, passed, base_other, added, result):
    half = passed.shape[1]
    for cols in columns(half):
        result[:, cols] = rounded(base_one[:, cols] + mixing(out_second[...], passed[:, cols]))
        at = slice(half + cols.start, half + cols.stop)
        result[:, at] = rounded(base_other[:, cols] + mixing(leaf_out[0], added[:, cols]))


def shards(sources, leaf_in, transfers, leaf_out, tile_mats, tile_list):
    levels_high = lax.axis_size("row").bit_length() - 1
    levels_low = lax.axis_size("col").bit_length() - 1
    hops = [("row", 1 << bit) for bit in range(levels_high)]
    hops += [("col", 1 << bit) for bit in range(levels_low)]
    last = len(hops) - 1
    rank, vecs = sources.shape
    half = vecs // 2
    bf16, f32 = jnp.bfloat16, jnp.float32
    live = tile_list.astype(f32)
    core = lax.axis_index("col").reshape(1) % 2

    coeffs = rounded(mixing(leaf_in[0], sources))

    low_bit, high_bit = hops[last - 1][1], hops[last][1]
    side_bit = low_bit ^ high_bit
    near = exchange(transfers[0, last - 1 :], "col", low_bit)
    at_side = exchange(jnp.stack([transfers[0, last - 1, 0], near[0, 1]]), "col", side_bit)

    (steps,) = local(near_products, [((2, rank, vecs), bf16)], [live, tile_mats, sources], 8, vecs)
    met = exchange(steps, "col", 1)
    down, up = local(near_meet, [((rank, vecs), bf16)] * 2, [core, live, tile_mats, sources, met], 8, vecs)
    above = from_behind(up, "col", 2)
    beneath = from_behind(down, "col", -2)

    for level in range(last - 1):
        axis, flip = hops[level]
        partner = exchange(coeffs, axis, flip)
        coeffs = rounded(mixing(transfers[0, level, 0], coeffs) + mixing(transfers[0, level, 1], partner))

    one, other = coeffs[:, :half], coeffs[:, half:]
    low = exchange(one, "col", low_bit)
    side = exchange(other, "col", side_bit)
    ready_one, ready_other, across, first = local(
        pair_ready,
        [((rank, half), f32), ((rank, half), f32), ((rank, rank), bf16), ((rank, rank), bf16)],
        [near, at_side, one, other],
        7,
    )
    (passed,) = local(pair_send, [((rank, half), bf16)], [first, ready_one, low], 1)
    passed = exchange(passed, "col", side_bit)
    (part,) = local(pair_send, [((rank, half), bf16)], [across, ready_other, side], 1)
    added = exchange(part, "col", low_bit)
    base_one, base_other, out_second = local(
        finish_base(last - 1),
        [((rank, half), f32), ((rank, half), f32), ((rank, rank), bf16)],
        [core, live, transfers, leaf_out, at_side, tile_mats, one, low, other, side, sources, met, above, beneath],
        23,
    )
    (result,) = local(finish, [((rank, vecs), bf16)], [out_second, leaf_out, base_one, passed, base_other, added], 4)
    return result


def solution(mesh):
    return jax.shard_map(
        shards,
        mesh=mesh,
        in_specs=(
            P(("row", "col"), None),
            P(("row", "col"), None, None),
            P(("row", "col"), None, None, None, None),
            P(("row", "col"), None, None),
            P(("row", "col"), None, None, None),
            P(("row", "col"), None),
        ),
        out_specs=P(("row", "col"), None),
        check_vma=False,
    )
```
